256 devices in a mesh: dp: 4 (over y), fsdp: 8 (over z), tensor: 8 (over x, core).
Axes of the slice: x: 4, y: 4, z: 8, core: 2. Of those that a mesh axis runs over, the one named last changes fastest.
Arguments:
- momentum: bfloat16 [4, 8192, 8192], P('dp', 'fsdp', 'tensor'), may hold values from -24 to 24
- gradient: bfloat16 [4, 8192, 8192], P('dp', 'fsdp', 'tensor'), may hold values from -4 to 4
- factor: float32 [8192, 256], P('tensor'), may hold values from -6 to 6
Outputs:
- new_momentum: float32 [4, 8192, 8192], P('dp', 'fsdp', 'tensor')
- step_direction: bfloat16 [8192, 8192], P('fsdp', 'tensor')
- new_factor: float32 [8192, 256], P('tensor')
The draws below stay inside these ranges and needn't reach their ends.
All inputs are finite; a program needn't handle non-finite values.
Results may differ from the reference program's by a relative error of at most 0.0065.
Values may be sent and summed in bfloat16 or wider, within the bound.
A program may use at most 64 MiB of HBM per device.

```python
import jax
import jax.numpy as jnp
from jax import lax

ROWS = 8192
COLS = 8192
RANK = 256
REPLICAS = 4


def rising_scale(key, count, start, finish, rough):
    trend = jnp.linspace(jnp.log(start), jnp.log(finish), count).astype(jnp.float32)
    jitter = jax.random.uniform(key, (count,), jnp.float32, jnp.log(rough), 0.0)
    return jnp.exp(trend + jitter)


def draw_momentum(key, part):
    low_rank = max(RANK // 2, 1)
    key_rows = jax.random.fold_in(key, 21)
    key_cols = jax.random.fold_in(key, 22)
    key_left = jax.random.fold_in(key, 23)
    key_right = jax.random.fold_in(key, 24)
    key_weights = jax.random.fold_in(key, 25)
    key_noise = jax.random.fold_in(key, 26)
    key_replica = jax.random.fold_in(key, 27)
    row_scale = rising_scale(key_rows, ROWS, 0.5, 4.0, 0.5)
    col_scale = rising_scale(key_cols, COLS, 0.5, 4.0, 0.5)
    left_basis = jax.random.normal(key_left, (ROWS, low_rank), jnp.float32)
    right_basis = jax.random.normal(key_right, (COLS, low_rank), jnp.float32)
    noise = jax.random.normal(key_noise, (REPLICAS, ROWS, COLS), jnp.float32)
    replica_scale = jnp.exp(jnp.linspace(0.0, jnp.log(3.0), REPLICAS).astype(jnp.float32) + jax.random.uniform(key_replica, (REPLICAS,), jnp.float32, -0.1, 0.1))
    weights = jnp.exp(jax.random.uniform(key_weights, (low_rank,), jnp.float32, 0.0, jnp.log(2.0)))
    shared = jnp.dot(left_basis * weights[None, :], right_basis.T) / jnp.sqrt(jnp.sum(weights * weights))
    values = shared[None] + noise
    values = 0.15 * values * replica_scale[:, None, None] * row_scale[None, :, None] * col_scale[None, None, :]
    return jnp.clip(values, -24.0, 24.0).astype(jnp.bfloat16)


def draw_gradient(key, part):
    key_rows = jax.random.fold_in(key, 11)
    key_cols = jax.random.fold_in(key, 12)
    key_own = jax.random.fold_in(key, 13)
    row_scale = jnp.exp(jax.random.uniform(key_rows, (1, ROWS, 1), jnp.float32, jnp.log(0.3), jnp.log(3.0)))
    col_scale = jnp.exp(jax.random.uniform(key_cols, (1, 1, COLS), jnp.float32, jnp.log(0.3), jnp.log(3.0)))
    values = jax.random.truncated_normal(key_own, -4.0, 4.0, (REPLICAS, ROWS, COLS), jnp.float32)
    return (0.1 * values * row_scale * col_scale).astype(jnp.bfloat16)


def shard_levels(rng, shape, pieces, least, largest):
    def one(dim, shards_of):
        heights = jax.random.uniform(jax.random.fold_in(jax.random.fold_in(rng, 6), dim), (shards_of,), jnp.float32, least / len(pieces), largest / len(pieces))
        return jnp.repeat(jnp.exp(heights), shape[dim] // shards_of).reshape((-1,) + (1,) * (len(shape) - dim - 1))

    gain = one(*pieces[0])
    for cut in pieces[1:]:
        gain = gain * one(*cut)
    return gain


def scatter_about(rng, shape, deviation, limit, shards=(), held_as=jnp.bfloat16):
    loudness = shard_levels(rng, shape, shards, -0.22, 0.18) if shards else 1.0
    array = jax.random.normal(rng, shape, jnp.float32) * deviation * loudness
    return jnp.minimum(jnp.maximum(array, -limit), limit).astype(held_as)


def setup_inputs(seed: int = 0) -> dict:
    arg_keys = jax.random.split(jax.random.key(seed), 4)
    return {
        "momentum": draw_momentum(jax.random.fold_in(arg_keys[3], 71), 0),
        "gradient": draw_gradient(jax.random.fold_in(arg_keys[3], 71), 0),
        "factor": scatter_about(arg_keys[2], (COLS, RANK), 1.0, 6.0, ((0, 8),), jnp.float32),
    }


def reference(momentum, gradient, factor):
    highest = lax.Precision.HIGHEST
    factor_low = factor.astype(jnp.bfloat16)
    left = jnp.zeros((ROWS, RANK), jnp.float32)
    for replica in range(REPLICAS):
        left = left + jnp.dot(momentum[replica].astype(jnp.float32), factor_low.astype(jnp.float32), preferred_element_type=jnp.float32)
        left = left + jnp.dot(gradient[replica].astype(jnp.float32), factor_low.astype(jnp.float32), preferred_element_type=jnp.float32)
    left = left / REPLICAS
    gram = jnp.dot(left.T, left, precision=highest)
    lower = jnp.linalg.cholesky(gram)
    ortho = jax.scipy.linalg.solve_triangular(lower, left.T, lower=True).T
    ortho_low = ortho.astype(jnp.bfloat16)
    right = jnp.zeros((COLS, RANK), jnp.float32)
    for replica in range(REPLICAS):
        right = right + jnp.dot(momentum[replica].T.astype(jnp.float32), ortho_low.astype(jnp.float32), preferred_element_type=jnp.float32)
        right = right + jnp.dot(gradient[replica].T.astype(jnp.float32), ortho_low.astype(jnp.float32), preferred_element_type=jnp.float32)
    right = right / REPLICAS
    square_sums = lax.optimization_barrier(jnp.sum(right * right, axis=0))
    new_factor = right / jnp.sqrt(square_sums / COLS + 1e-06)
    right_low = right.astype(jnp.bfloat16)
    feedback = jnp.dot(ortho_low.astype(jnp.float32), right_low.T.astype(jnp.float32), preferred_element_type=jnp.float32)
    new_momentum = jnp.stack([momentum[replica].astype(jnp.float32) + gradient[replica].astype(jnp.float32) - 0.05 * feedback for replica in range(REPLICAS)])
    step_scale = jnp.sqrt(jnp.float32(ROWS / RANK))
    factor_next_low = new_factor.astype(jnp.bfloat16)
    step_direction = (step_scale * jnp.dot(ortho_low.astype(jnp.float32), factor_next_low.T.astype(jnp.float32), preferred_element_type=jnp.float32)).astype(jnp.bfloat16)
    return (new_momentum, step_direction, new_factor)
```

```python
import jax
import jax.numpy as jnp
from jax import lax
from jax.experimental import pallas as pl
from jax.experimental.pallas import tpu as pltpu
from jax.sharding import PartitionSpec as P

ROWS = 8192
COLS = 8192
RANK = 256

MESH = pl.DeviceIdType.MESH
HIGHEST = lax.Precision.HIGHEST
F32 = jnp.float32
BF16 = jnp.bfloat16
BLOCK = 64
BLOCKS = RANK // BLOCK
Y, Z, X = 4, 8, 4
CHIPS = X * Y
PLANE = Y * Z
LOCAL = 1024
HALF = LOCAL // 2
OWN = LOCAL // (2 * CHIPS)
PARTS = 8
CHUNK = LOCAL // PARTS
QUARTER = LOCAL // Y


def dot(a, b):
    return jnp.dot(a, b, precision=HIGHEST, preferred_element_type=F32)


def low_dot(a, b):
    return jnp.dot(a, b, preferred_element_type=F32)


def factor_block(w, size):
    lanes = w.shape[1]
    row = lax.broadcasted_iota(jnp.int32, (8, lanes), 0)
    done = []
    for j in range(0, size, 8):
        v = w[0:8, :]
        p = [jnp.broadcast_to(v[m : m + 1, :], (8, lanes)) for m in range(8)]
        a = [
            [jnp.broadcast_to(p[i][:, j + m : j + m + 1], (8, lanes)) for m in range(i + 1)]
            for i in range(8)
        ]
        rest = w[8:, :]
        n = rest.shape[0]
        columns = [jnp.broadcast_to(rest[:, j + m : j + m + 1], (n, lanes)) for m in range(8)] if n else []
        low = [[None] * 8 for _ in range(8)]
        inverse = [None] * 8
        for k in range(8):
            inverse[k] = 1.0 / a[k][k]
            for i in range(k + 1, 8):
                low[i][k] = a[i][k] * inverse[k]
            for i in range(k + 1, 8):
                for m in range(k + 1, i + 1):
                    a[i][m] = a[i][m] - low[i][k] * a[m][k]
            for i in range(k + 1, 8):
                p[i] = p[i] - low[i][k] * p[k]
        out = p[7] * lax.rsqrt(a[7][7])
        for k in range(6, -1, -1):
            out = jnp.where(row == k, p[k] * lax.rsqrt(a[k][k]), out)
        done.append(out)
        if n:
            q = [None] * 8
            for k in range(7, -1, -1):
                q[k] = p[k] * inverse[k]
                for i in range(7, k, -1):
                    q[k] = q[k] - low[i][k] * q[i]
            for k in range(8):
                rest = rest - columns[k] * jnp.broadcast_to(q[k][0:1, :], (n, lanes))
            w = rest
    return jnp.concatenate(done, axis=0)


def eliminate(gram, inv, block):
    lo, hi = block * BLOCK, (block + 1) * BLOCK
    rows = gram[lo:hi, :]
    r_i = lax.broadcasted_iota(jnp.int32, (BLOCK, BLOCK), 0)
    c_i = lax.broadcasted_iota(jnp.int32, (BLOCK, BLOCK), 1)
    eye = jnp.where(r_i == c_i, 1.0, 0.0).astype(F32)
    root = factor_block(jnp.concatenate([rows[:, lo:hi], eye], axis=1), BLOCK)[:, BLOCK:]
    mine = dot(root, inv[lo:hi, :])
    inv[lo:hi, :] = mine
    if hi < RANK:
        upper = dot(root, rows)
        below = upper.T[hi:, :]
        gram[hi:, :] = gram[hi:, :] - dot(below, upper)
        inv[hi:, :] = inv[hi:, :] - dot(below, mine)
    return mine


def remote(src, dst, send, recv, **where):
    return pltpu.make_async_remote_copy(
        src_ref=src, dst_ref=dst, send_sem=send, recv_sem=recv, device_id=where, device_id_type=MESH
    )


def take(ref, sem):
    pltpu.make_async_copy(ref, ref, sem).wait()


def core_kernel(
    m_hbm, g_hbm, f_ref,
    ortho_t, right_t, squares,
    mv, gv, fv, part, partner_in, half, outgoing, incoming, left, left_t,
    gram, gram_in, gram_all, work, inv, rs_out, rs_in, spread, square_in,
    load_sem, pair_sem, rs_sem, ag_send, ag_recv, fw_send, fw_recv,
    z_sem, gg_send, gg_recv, gf_send, gf_recv, r_send, r_recv, s_send, s_recv, n_sem,
):
    y = lax.axis_index("dp")
    z = lax.axis_index("fsdp")
    t = lax.axis_index("tensor")
    x = t // 2
    c = lax.rem(t, 2)
    other = t + 1 - 2 * c
    chip = y * X + x
    me = c * CHIPS + chip

    def first_row(i):
        half_of = jnp.where(i < PARTS // 2, 1 - c, c)
        return pl.multiple_of(half_of * HALF + lax.rem(i, PARTS // 2) * CHUNK, CHUNK)

    def load(i, which):
        src, dst = ((m_hbm, mv), (g_hbm, gv))[which]
        rows = pl.ds(first_row(i), CHUNK)
        return pltpu.make_async_copy(src.at[rows, :], dst.at[rows, :], load_sem.at[which, i])

    for i in range(PARTS):
        load(i, 0).start()
        load(i, 1).start()

    def chip_at(d):
        return lax.rem(y + d // X, Y), lax.rem(x + lax.rem(d, X), X)

    def line_at(d):
        return lax.rem(y + d // Z, Y), lax.rem(z + lax.rem(d, Z), Z)

    barrier = pltpu.get_barrier_semaphore()

    @pl.loop(1, CHIPS)
    def _(d):
        py, px = chip_at(d)
        pl.semaphore_signal(barrier, inc=1, device_id={"dp": py, "fsdp": z, "tensor": px * 2 + c}, device_id_type=MESH)

    @pl.loop(1, PLANE)
    def _(d):
        py, pz = line_at(d)
        pl.semaphore_signal(barrier, inc=1, device_id={"dp": py, "fsdp": pz, "tensor": t}, device_id_type=MESH)

    @pl.loop(1, 2 * X)
    def _(d):
        pl.semaphore_signal(barrier, inc=1, device_id={"dp": y, "fsdp": z, "tensor": lax.rem(t + d, 2 * X)}, device_id_type=MESH)

    fv[...] = f_ref[...].astype(BF16)

    def product(i):
        load(i, 0).wait()
        load(i, 1).wait()
        rows = pl.ds(first_row(i), CHUNK)
        part[pl.ds(pl.multiple_of(i * CHUNK, CHUNK), CHUNK), :] = low_dot(mv[rows, :], fv[...]) + low_dot(gv[rows, :], fv[...])

    @pl.loop(0, PARTS // 2)
    def _(i):
        product(i)

    pl.semaphore_wait(barrier, CHIPS - 1 + PLANE - 1 + 2 * X - 1)
    to_partner = remote(part.at[0:HALF, :], partner_in, pair_sem.at[0], pair_sem.at[1], dp=y, fsdp=z, tensor=other)
    to_partner.start()

    @pl.loop(PARTS // 2, PARTS)
    def _(i):
        product(i)

    to_partner.wait_recv()
    total = (part[HALF:, :] + partner_in[...]).reshape(CHIPS, OWN, RANK)
    half[...] = total
    outgoing[...] = total.astype(BF16)

    @pl.loop(1, CHIPS)
    def _(d):
        py, px = chip_at(d)
        remote(outgoing.at[py * X + px], incoming.at[d], rs_sem.at[0], rs_sem.at[1], dp=py, fsdp=z, tensor=px * 2 + c).start()

    take(incoming.at[1:], rs_sem.at[1])
    mine = half[chip]
    for d in range(1, CHIPS):
        mine = mine + incoming[d].astype(F32)
    left[me] = mine * 0.25

    def left_copy(d):
        py, px = chip_at(d)
        return remote(left.at[me], left.at[me], ag_send.at[d], ag_recv.at[d], dp=py, fsdp=z, tensor=px * 2 + c)

    def left_forward(d):
        py, px = lax.rem(y + Y - d // X, Y), lax.rem(x + X - lax.rem(d, X), X)
        slot = c * CHIPS + py * X + px
        return remote(left.at[slot], left.at[slot], fw_send.at[d], fw_recv.at[d], dp=y, fsdp=z, tensor=other)

    @pl.loop(1, CHIPS)
    def _(d):
        left_copy(d).start()

    left_forward(0).start()

    @pl.loop(1, CHIPS)
    def _(d):
        left_copy(d).wait_recv()
        left_forward(d).start()

    @pl.loop(0, CHIPS)
    def _(d):
        left_forward(d).wait_recv()

    rows = left[...].reshape(LOCAL, RANK)
    left_t[...] = rows.T
    gram[...] = dot(left_t[...], rows).reshape(2 * CHIPS, 8, RANK)

    @pl.loop(1, Z)
    def _(d):
        remote(gram.at[me], gram_in.at[d], z_sem.at[0], z_sem.at[1], dp=y, fsdp=lax.rem(z + d, Z), tensor=t).start()

    take(gram_in.at[1:], z_sem.at[1])
    mine = gram[me]
    for d in range(1, Z):
        mine = mine + gram_in[d]
    gram_all[me] = mine

    def gram_copy(d):
        py, px = chip_at(d)
        return remote(gram_all.at[me], gram_all.at[me], gg_send.at[d], gg_recv.at[d], dp=py, fsdp=z, tensor=px * 2 + c)

    def gram_forward(d):
        py, px = lax.rem(y + Y - d // X, Y), lax.rem(x + X - lax.rem(d, X), X)
        slot = c * CHIPS + py * X + px
        return remote(gram_all.at[slot], gram_all.at[slot], gf_send.at[d], gf_recv.at[d], dp=y, fsdp=z, tensor=other)

    @pl.loop(1, CHIPS)
    def _(d):
        gram_copy(d).start()

    gram_forward(0).start()

    @pl.loop(1, CHIPS)
    def _(d):
        gram_copy(d).wait_recv()
        gram_forward(d).start()

    @pl.loop(0, CHIPS)
    def _(d):
        gram_forward(d).wait_recv()

    work[...] = gram_all[...].reshape(RANK, RANK)
    r_i = lax.broadcasted_iota(jnp.int32, (RANK, RANK), 0)
    c_i = lax.broadcasted_iota(jnp.int32, (RANK, RANK), 1)
    inv[...] = jnp.where(r_i == c_i, 1.0, 0.0).astype(F32)

    def right_send(b):
        @pl.loop(1, PLANE)
        def _(d):
            py, pz = line_at(d)
            remote(rs_out.at[b, py * Z + pz], rs_in.at[b, d], r_send.at[b], r_recv.at[b], dp=py, fsdp=pz, tensor=t).start()

    def right_sum(b):
        take(rs_in.at[b, 1:], r_recv.at[b])
        mine = rs_out[b, y * Z + z].astype(F32)
        for d in range(1, PLANE):
            mine = mine + rs_in[b, d].astype(F32)
        spread[b, y * Z + z] = (mine * 0.25).astype(BF16)

        @pl.loop(1, PLANE)
        def _(d):
            py, pz = line_at(d)
            slot = spread.at[b, y * Z + z]
            remote(slot, slot, s_send.at[b], s_recv.at[b], dp=py, fsdp=pz, tensor=t).start()

    for b in range(BLOCKS):
        rows_of = eliminate(work, inv, b)
        low = dot(rows_of, left_t[...]).astype(BF16)
        ortho_t[b * BLOCK : (b + 1) * BLOCK, :] = low
        term = low_dot(low, mv[...]) + low_dot(low, gv[...])
        for pz in range(Z):
            for py in range(Y):
                rs_out[b, py * Z + pz] = term[pz * 8 : pz * 8 + 8, py * QUARTER : (py + 1) * QUARTER].astype(BF16)
        right_send(b)
        if b:
            right_sum(b - 1)
    right_sum(BLOCKS - 1)

    sums = jnp.zeros((8, RANK), F32)
    for b in range(BLOCKS):
        take(spread.at[b, 1:], s_recv.at[b])
        for py in range(Y):
            for pz in range(0, Z, 2):
                two = jnp.concatenate([spread[b, py * Z + pz], spread[b, py * Z + pz + 1]], axis=0)
                right_t[b * BLOCK + pz * 8 : b * BLOCK + pz * 8 + 16, py * QUARTER : (py + 1) * QUARTER] = two
    full = right_t[...].astype(F32)
    ones = jnp.ones((8, LOCAL), F32)
    square_in[t] = lax.dot_general(ones, full * full, (((1,), (1,)), ((), ())), precision=HIGHEST, preferred_element_type=F32)

    @pl.loop(1, 2 * X)
    def _(d):
        remote(square_in.at[t], square_in.at[t], n_sem.at[0], n_sem.at[1], dp=y, fsdp=z, tensor=lax.rem(t + d, 2 * X)).start()

    take(square_in.at[1:], n_sem.at[1])
    sums = square_in[0]
    for d in range(1, 2 * X):
        sums = sums + square_in[d]
    squares[...] = sums

    to_partner.wait_send()
    take(outgoing.at[1:], rs_sem.at[0])

    @pl.loop(1, CHIPS)
    def _(d):
        left_copy(d).wait_send()
        gram_copy(d).wait_send()

    @pl.loop(0, CHIPS)
    def _(d):
        left_forward(d).wait_send()
        gram_forward(d).wait_send()

    take(gram_in.at[1:], z_sem.at[0])
    for b in range(BLOCKS):
        take(rs_out.at[b, 1:], r_send.at[b])
        take(spread.at[b, 1:], s_send.at[b])
    take(square_in.at[1:], n_sem.at[0])


def core(moment, change, factor):
    vmem = pl.BlockSpec(memory_space=pltpu.VMEM)
    hbm = pl.BlockSpec(memory_space=pl.ANY)
    dma = pltpu.SemaphoreType.DMA
    return pl.pallas_call(
        core_kernel,
        out_shape=(
            jax.ShapeDtypeStruct((RANK, LOCAL), BF16),
            jax.ShapeDtypeStruct((RANK, LOCAL), BF16),
            jax.ShapeDtypeStruct((8, RANK), F32),
        ),
        in_specs=[hbm, hbm, vmem],
        out_specs=(vmem, vmem, vmem),
        scratch_shapes=[
            pltpu.VMEM((LOCAL, LOCAL), BF16),
            pltpu.VMEM((LOCAL, LOCAL), BF16),
            pltpu.VMEM((LOCAL, RANK), BF16),
            pltpu.VMEM((LOCAL, RANK), F32),
            pltpu.VMEM((HALF, RANK), F32),
            pltpu.VMEM((CHIPS, OWN, RANK), F32),
            pltpu.VMEM((CHIPS, OWN, RANK), BF16),
            pltpu.VMEM((CHIPS, OWN, RANK), BF16),
            pltpu.VMEM((2 * CHIPS, OWN, RANK), F32),
            pltpu.VMEM((RANK, LOCAL), F32),
            pltpu.VMEM((2 * CHIPS, 8, RANK), F32),
            pltpu.VMEM((Z, 8, RANK), F32),
            pltpu.VMEM((2 * CHIPS, 8, RANK), F32),
            pltpu.VMEM((RANK, RANK), F32),
            pltpu.VMEM((RANK, RANK), F32),
            pltpu.VMEM((BLOCKS, PLANE, 8, QUARTER), BF16),
            pltpu.VMEM((BLOCKS, PLANE, 8, QUARTER), BF16),
            pltpu.VMEM((BLOCKS, PLANE, 8, QUARTER), BF16),
            pltpu.VMEM((2 * X, 8, RANK), F32),
            dma((2, PARTS)),
            dma((2,)),
            dma((2,)),
            dma((CHIPS,)),
            dma((CHIPS,)),
            dma((CHIPS,)),
            dma((CHIPS,)),
            dma((2,)),
            dma((CHIPS,)),
            dma((CHIPS,)),
            dma((CHIPS,)),
            dma((CHIPS,)),
            dma((BLOCKS,)),
            dma((BLOCKS,)),
            dma((BLOCKS,)),
            dma((BLOCKS,)),
            dma((2,)),
        ],
        compiler_params=pltpu.CompilerParams(
            collective_id=0, has_side_effects=True, vmem_limit_bytes=48 * 1024 * 1024
        ),
    )(moment, change, factor)


def final_kernel(m_ref, g_ref, o_ref, r_ref, r_part, s_ref, nm_ref, sd_ref, nf_ref, fv, iv):
    @pl.when(pl.program_id(0) == 0)
    def _():
        scale = lax.rsqrt(s_ref[...] * (1.0 / COLS) + 1e-06)
        iv[...] = jnp.broadcast_to(scale.T[:, 0:1], (RANK, 128))
        fv[...] = (r_ref[...].astype(F32) * iv[:, 0:1]).astype(BF16)

    across = (((0,), (0,)), ((), ()))
    ortho = o_ref[...].astype(F32).T.astype(BF16)
    feedback = low_dot(ortho, r_ref[...])
    nm_ref[...] = m_ref[...].astype(F32) + g_ref[...].astype(F32) - 0.05 * feedback
    sd_ref[...] = (jnp.sqrt(F32(ROWS / RANK)) * low_dot(ortho, fv[...])).astype(BF16)
    nf_ref[...] = (r_part[...].astype(F32) * iv[...]).T


def final(moment, change, ortho_t, right_t, squares):
    step = 128
    row = lambda i: (i, 0)
    col = lambda i: (0, i)
    fixed = lambda i: (0, 0)
    return pl.pallas_call(
        final_kernel,
        grid=(LOCAL // step,),
        out_shape=(
            jax.ShapeDtypeStruct((LOCAL, LOCAL), F32),
            jax.ShapeDtypeStruct((LOCAL, LOCAL), BF16),
            jax.ShapeDtypeStruct((LOCAL, RANK), F32),
        ),
        in_specs=[
            pl.BlockSpec((step, LOCAL), row),
            pl.BlockSpec((step, LOCAL), row),
            pl.BlockSpec((RANK, step), col),
            pl.BlockSpec((RANK, LOCAL), fixed),
            pl.BlockSpec((RANK, step), col),
            pl.BlockSpec((8, RANK), fixed),
        ],
        out_specs=(
            pl.BlockSpec((step, LOCAL), row),
            pl.BlockSpec((step, LOCAL), row),
            pl.BlockSpec((step, RANK), row),
        ),
        scratch_shapes=[pltpu.VMEM((RANK, LOCAL), BF16), pltpu.VMEM((RANK, 128), F32)],
    )(moment, change, ortho_t, right_t, right_t, squares)


def local(momentum, gradient, factor):
    ortho_t, right_t, squares = core(momentum[0], gradient[0], factor)
    new_momentum, step_direction, new_factor = final(momentum[0], gradient[0], ortho_t, right_t, squares)
    return new_momentum[None], step_direction, new_factor


def solution(mesh):
    in_specs = (P("dp", "fsdp", "tensor"), P("dp", "fsdp", "tensor"), P("tensor", None))
    out_specs = (P("dp", "fsdp", "tensor"), P("fsdp", "tensor"), P("tensor", None))
    return jax.shard_map(local, mesh=mesh, in_specs=in_specs, out_specs=out_specs, check_vma=False)
```

```python
import jax
import jax.numpy as jnp
from jax import lax
from jax.experimental import pallas as pl
from jax.experimental.pallas import tpu as pltpu
from jax.sharding import PartitionSpec as P

ROWS = 8192
COLS = 8192
RANK = 256

MESH = pl.DeviceIdType.MESH
HIGHEST = lax.Precision.HIGHEST
F32 = jnp.float32
BF16 = jnp.bfloat16
BLOCK = 64
BLOCKS = RANK // BLOCK
Y, Z, X = 4, 8, 4
STOP = 99
CORE_MIB = 52
FINAL_MIB = 24
CHIPS = X * Y
PLANE = Y * Z
LOCAL = 1024
HALF = LOCAL // 2
OWN = LOCAL // (2 * CHIPS)
PARTS = 8
CHUNK = LOCAL // PARTS
TILE = 128
QUARTER = LOCAL // Y


def dot(a, b):
    return jnp.dot(a, b, precision=HIGHEST, preferred_element_type=F32)


def low_dot(a, b):
    return jnp.dot(a, b, preferred_element_type=F32)


def factor_block(w, size):
    lanes = w.shape[1]
    row = lax.broadcasted_iota(jnp.int32, (8, lanes), 0)
    done = []
    for j in range(0, size, 8):
        v = w[0:8, :]
        p = [jnp.broadcast_to(v[m : m + 1, :], (8, lanes)) for m in range(8)]
        a = [
            [jnp.broadcast_to(p[i][:, j + m : j + m + 1], (8, lanes)) for m in range(i + 1)]
            for i in range(8)
        ]
        rest = w[8:, :]
        n = rest.shape[0]
        columns = [jnp.broadcast_to(rest[:, j + m : j + m + 1], (n, lanes)) for m in range(8)] if n else []
        low = [[None] * 8 for _ in range(8)]
        inverse = [None] * 8
        for k in range(8):
            inverse[k] = 1.0 / a[k][k]
            for i in range(k + 1, 8):
                low[i][k] = a[i][k] * inverse[k]
            for i in range(k + 1, 8):
                for m in range(k + 1, i + 1):
                    a[i][m] = a[i][m] - low[i][k] * a[m][k]
            for i in range(k + 1, 8):
                p[i] = p[i] - low[i][k] * p[k]
        out = p[7] * lax.rsqrt(a[7][7])
        for k in range(6, -1, -1):
            out = jnp.where(row == k, p[k] * lax.rsqrt(a[k][k]), out)
        done.append(out)
        if n:
            q = [None] * 8
            for k in range(7, -1, -1):
                q[k] = p[k] * inverse[k]
                for i in range(7, k, -1):
                    q[k] = q[k] - low[i][k] * q[i]
            for k in range(8):
                rest = rest - columns[k] * jnp.broadcast_to(q[k][0:1, :], (n, lanes))
            w = rest
    return jnp.concatenate(done, axis=0)


def eliminate(gram, inv, block):
    lo, hi = block * BLOCK, (block + 1) * BLOCK
    rows = gram[lo:hi, :]
    r_i = lax.broadcasted_iota(jnp.int32, (BLOCK, BLOCK), 0)
    c_i = lax.broadcasted_iota(jnp.int32, (BLOCK, BLOCK), 1)
    eye = jnp.where(r_i == c_i, 1.0, 0.0).astype(F32)
    root = factor_block(jnp.concatenate([rows[:, lo:hi], eye], axis=1), BLOCK)[:, BLOCK:]
    mine = dot(root, inv[lo:hi, :])
    inv[lo:hi, :] = mine
    if hi < RANK:
        upper = dot(root, rows)
        below = upper.T[hi:, :]
        gram[hi:, :] = gram[hi:, :] - dot(below, upper)
        inv[hi:, :] = inv[hi:, :] - dot(below, mine)
    return mine


def remote(src, dst, send, recv, **where):
    return pltpu.make_async_remote_copy(
        src_ref=src, dst_ref=dst, send_sem=send, recv_sem=recv, device_id=where, device_id_type=MESH
    )


def take(ref, sem):
    pltpu.make_async_copy(ref, ref, sem).wait()


def hops(step, size):
    return min(step, size - step)


def by_distance(*sizes):
    steps = [()]
    for size in sizes:
        steps = [s + (i,) for s in steps for i in range(size)]
    far = lambda s: sum(hops(a, n) for a, n in zip(s, sizes) if n > 2)
    return sorted([s for s in steps if any(s)], key=far, reverse=True)


CHIP_STEPS = by_distance(Y, X)
PLANE_STEPS = by_distance(Y, X, 2)
LINE_STEPS = by_distance(Y, Z)
Z_STEPS = by_distance(Z)
X_STEPS = by_distance(X, 2)


def core_kernel(
    m_hbm, g_hbm, f_hbm,
    ortho, right_t, scale,
    mv, gv, ff, fv, part, partner_in, half, outgoing, incoming, left, left_t,
    gram, gram_in, line_in, gram_all, work, inv, rs_out, rs_in, spread, square_in,
    load_sem, pair_sem, rs_sem, ag_send, ag_recv, fw_send, fw_recv, gr_sem,
    z_sem, gg_send, gg_recv, gf_send, gf_recv, r_send, r_recv, s_send, s_recv, n_send, n_recv,
):
    y = lax.axis_index("dp")
    z = lax.axis_index("fsdp")
    t = lax.axis_index("tensor")
    x = t // 2
    c = lax.rem(t, 2)
    other = t + 1 - 2 * c
    me = c * CHIPS + y * X + x
    seat = y * Z + z
    own_base = c * HALF
    other_base = HALF - own_base

    def first_row(i):
        base = other_base if i < PARTS // 2 else own_base
        return pl.multiple_of(base + (i % (PARTS // 2)) * CHUNK, CHUNK)

    def load(i, which):
        src, dst = ((m_hbm, mv), (g_hbm, gv))[which]
        rows = pl.ds(first_row(i), CHUNK)
        return pltpu.make_async_copy(src.at[rows, :], dst.at[rows, :], load_sem.at[which, i])

    load_factor = pltpu.make_async_copy(f_hbm, ff, load_sem.at[2, 0])
    load_factor.start()
    for i in range(PARTS):
        load(i, 0).start()
        load(i, 1).start()

    def wrap(a, step, size):
        return lax.rem(a + step, size) if step else a

    def chip_at(step, back=False):
        dy, dx = step
        if back:
            dy, dx = (Y - dy) % Y, (X - dx) % X
        return wrap(y, dy, Y), wrap(x, dx, X)

    barrier = pltpu.get_barrier_semaphore()

    def greet(**where):
        pl.semaphore_signal(barrier, inc=1, device_id=where, device_id_type=MESH)

    for dy, dz in LINE_STEPS:
        greet(dp=wrap(y, dy, Y), fsdp=wrap(z, dz, Z), tensor=t)
    for dy, dx, dc in PLANE_STEPS:
        greet(dp=wrap(y, dy, Y), fsdp=z, tensor=wrap(x, dx, X) * 2 + wrap(c, dc, 2))

    pending = []

    def finish():
        for wait in pending:
            wait()

    load_factor.wait()
    fv[...] = ff[...].astype(BF16)
    for i in range(PARTS):
        load(i, 0).wait()
        load(i, 1).wait()
        rows = pl.ds(first_row(i), CHUNK)
        part[i * CHUNK : (i + 1) * CHUNK, :] = low_dot(mv[rows, :], fv[...]) + low_dot(gv[rows, :], fv[...])

    pl.semaphore_wait(barrier, len(LINE_STEPS) + len(PLANE_STEPS))
    if STOP == 1:
        return finish()
    to_partner = remote(part.at[0:HALF, :], partner_in, pair_sem.at[0], pair_sem.at[1], dp=y, fsdp=z, tensor=other)
    to_partner.start()
    pending.append(to_partner.wait_send)
    to_partner.wait_recv()
    both = (part[HALF:, :] + partner_in[...]).reshape(CHIPS, OWN, RANK)
    half[...] = both
    outgoing[...] = both.astype(BF16)

    for i, step in enumerate(CHIP_STEPS):
        py, px = chip_at(step)
        remote(outgoing.at[py * X + px], incoming.at[i], rs_sem.at[0], rs_sem.at[1], dp=py, fsdp=z, tensor=px * 2 + c).start()
    pending.append(lambda: take(incoming, rs_sem.at[0]))
    take(incoming, rs_sem.at[1])
    if STOP == 2:
        return finish()
    mine = half[y * X + x]
    for i in range(CHIPS - 1):
        mine = mine + incoming[i].astype(F32)
    mine = mine * 0.25
    left[me] = mine

    gram[...] = dot(mine.T, mine).reshape(2 * CHIPS, 8, RANK)
    for i, (dy, dx, dc) in enumerate(PLANE_STEPS):
        py, px, pc = wrap(y, dy, Y), wrap(x, dx, X), wrap(c, dc, 2)
        remote(gram.at[pc * CHIPS + py * X + px], gram_in.at[i], gr_sem.at[0], gr_sem.at[1], dp=py, fsdp=z, tensor=px * 2 + pc).start()
    pending.append(lambda: take(gram_in, gr_sem.at[0]))

    left_copies = []
    for i, step in enumerate(CHIP_STEPS):
        py, px = chip_at(step)
        copy = remote(left.at[me], left.at[me], ag_send.at[i], ag_recv.at[i], dp=py, fsdp=z, tensor=px * 2 + c)
        copy.start()
        left_copies.append(copy)
        pending.append(copy.wait_send)

    def forward(ref, send, recv, i, step):
        py, px = chip_at(step, back=True)
        slot = c * CHIPS + py * X + px
        copy = remote(ref.at[slot], ref.at[slot], send.at[i], recv.at[i], dp=y, fsdp=z, tensor=other)
        copy.start()
        pending.append(copy.wait_send)
        return copy

    left_forwards = [forward(left, fw_send, fw_recv, CHIPS - 1, (0, 0))]

    take(gram_in, gr_sem.at[1])
    if STOP == 3:
        for copy in left_copies:
            copy.wait_recv()
        left_forwards[0].wait_recv()
        return finish()
    mine = gram[me]
    for i in range(2 * CHIPS - 1):
        mine = mine + gram_in[i]
    gram[me] = mine

    for i, (dz,) in enumerate(Z_STEPS):
        remote(gram.at[me], line_in.at[i], z_sem.at[0], z_sem.at[1], dp=y, fsdp=wrap(z, dz, Z), tensor=t).start()
    pending.append(lambda: take(line_in, z_sem.at[0]))
    take(line_in, z_sem.at[1])
    for i in range(Z - 1):
        mine = mine + line_in[i]
    gram_all[me] = mine

    gram_copies = []
    for i, step in enumerate(CHIP_STEPS):
        py, px = chip_at(step)
        copy = remote(gram_all.at[me], gram_all.at[me], gg_send.at[i], gg_recv.at[i], dp=py, fsdp=z, tensor=px * 2 + c)
        copy.start()
        gram_copies.append(copy)
        pending.append(copy.wait_send)
    gram_forwards = [forward(gram_all, gf_send, gf_recv, CHIPS - 1, (0, 0))]
    if STOP == 4:
        for copy in left_copies + gram_copies:
            copy.wait_recv()
        left_forwards[0].wait_recv()
        gram_forwards[0].wait_recv()
        return finish()

    for i in range(CHIPS - 2, -1, -1):
        left_copies[i].wait_recv()
        left_forwards.append(forward(left, fw_send, fw_recv, i, CHIP_STEPS[i]))
    for copy in left_forwards:
        copy.wait_recv()
    left_t[...] = left[...].reshape(LOCAL, RANK).T
    for i in range(CHIPS - 2, -1, -1):
        gram_copies[i].wait_recv()
        gram_forwards.append(forward(gram_all, gf_send, gf_recv, i, CHIP_STEPS[i]))
    for copy in gram_forwards:
        copy.wait_recv()
    if STOP == 5:
        return finish()

    work[...] = gram_all[...].reshape(RANK, RANK)
    r_i = lax.broadcasted_iota(jnp.int32, (RANK, RANK), 0)
    c_i = lax.broadcasted_iota(jnp.int32, (RANK, RANK), 1)
    inv[...] = jnp.where(r_i == c_i, 1.0, 0.0).astype(F32)

    def right_sum(b):
        take(rs_in.at[b], r_recv.at[b])
        mine = rs_out[b, seat].astype(F32)
        for i in range(PLANE - 1):
            mine = mine + rs_in[b, i].astype(F32)
        spread[b, seat] = (mine * 0.25).astype(BF16)
        slot = spread.at[b, seat]
        for dy, dz in LINE_STEPS:
            remote(slot, slot, s_send.at[b], s_recv.at[b], dp=wrap(y, dy, Y), fsdp=wrap(z, dz, Z), tensor=t).start()
        pending.append(lambda: take(rs_in.at[b], s_send.at[b]))

    k_i = lax.broadcasted_iota(jnp.int32, (BLOCK, TILE), 0)
    l_i = lax.broadcasted_iota(jnp.int32, (BLOCK, TILE), 1)

    def collect(b):
        take(rs_in.at[b], s_recv.at[b])
        squares = jnp.zeros((BLOCK, QUARTER), F32)
        for py in range(Y):
            piece = jnp.concatenate([spread[b, py * Z + pz].astype(F32) for pz in range(Z)], axis=0)
            right_t[b * BLOCK : (b + 1) * BLOCK, py * QUARTER : (py + 1) * QUARTER] = piece.astype(BF16)
            squares = squares + piece * piece
        column = jnp.sum(squares, axis=1, keepdims=True)
        line = jnp.sum(jnp.where(k_i == l_i, column, 0.0), axis=0, keepdims=True)
        square_in[b, t] = jnp.broadcast_to(line, (8, TILE))
        for dx, dc in X_STEPS:
            slot = square_in.at[b, t]
            remote(slot, slot, n_send.at[b], n_recv.at[b], dp=y, fsdp=z, tensor=wrap(x, dx, X) * 2 + wrap(c, dc, 2)).start()
        pending.append(lambda: take(square_in.at[b, 1:], n_send.at[b]))

    def norm(b):
        take(square_in.at[b, 1:], n_recv.at[b])
        sums = square_in[b, 0]
        for i in range(1, 2 * X):
            sums = sums + square_in[b, i]
        column = jnp.sum(jnp.where(k_i == l_i, sums[0:1, :], 0.0), axis=1, keepdims=True)
        scale[b * BLOCK : (b + 1) * BLOCK, :] = jnp.broadcast_to(lax.rsqrt(column * (1.0 / COLS) + 1e-06), (BLOCK, TILE))

    for b in range(BLOCKS):
        rows_of = eliminate(work, inv, b)
        wide = dot(rows_of, left_t[...])
        low = wide.astype(BF16)
        term = low_dot(low, mv[...]) + low_dot(low, gv[...])
        for pz in range(Z):
            for py in range(Y):
                rs_out[b, py * Z + pz] = term[pz * 8 : pz * 8 + 8, py * QUARTER : (py + 1) * QUARTER].astype(BF16)
        for i, (dy, dz) in enumerate(LINE_STEPS):
            py, pz = wrap(y, dy, Y), wrap(z, dz, Z)
            remote(rs_out.at[b, py * Z + pz], rs_in.at[b, i], r_send.at[b], r_recv.at[b], dp=py, fsdp=pz, tensor=t).start()
        pending.append(lambda b=b: take(rs_in.at[b], r_send.at[b]))
        ortho[:, b * BLOCK : (b + 1) * BLOCK] = wide.T.astype(BF16)
        if b >= 2:
            right_sum(b - 2)
    if STOP == 6:
        for b in (2, 3):
            take(rs_in.at[b], r_recv.at[b])
        for b in (0, 1):
            take(rs_in.at[b], s_recv.at[b])
        return finish()
    collect(0)
    right_sum(2)
    collect(1)
    norm(0)
    right_sum(3)
    collect(2)
    norm(1)
    norm(2)
    if STOP == 7:
        take(rs_in.at[3], s_recv.at[3])
        return finish()
    collect(3)
    norm(3)
    finish()


def core(moment, change, factor):
    vmem = pl.BlockSpec(memory_space=pltpu.VMEM)
    hbm = pl.BlockSpec(memory_space=pltpu.HBM)
    dma = pltpu.SemaphoreType.DMA
    return pl.pallas_call(
        core_kernel,
        out_shape=(
            jax.ShapeDtypeStruct((LOCAL, RANK), BF16),
            jax.ShapeDtypeStruct((RANK, LOCAL), BF16),
            jax.ShapeDtypeStruct((RANK, TILE), F32),
        ),
        in_specs=[hbm, hbm, hbm],
        out_specs=(vmem, vmem, vmem),
        scratch_shapes=[
            pltpu.VMEM((LOCAL, LOCAL), BF16),
            pltpu.VMEM((LOCAL, LOCAL), BF16),
            pltpu.VMEM((LOCAL, RANK), F32),
            pltpu.VMEM((LOCAL, RANK), BF16),
            pltpu.VMEM((LOCAL, RANK), F32),
            pltpu.VMEM((HALF, RANK), F32),
            pltpu.VMEM((CHIPS, OWN, RANK), F32),
            pltpu.VMEM((CHIPS, OWN, RANK), BF16),
            pltpu.VMEM((CHIPS - 1, OWN, RANK), BF16),
            pltpu.VMEM((2 * CHIPS, OWN, RANK), F32),
            pltpu.VMEM((RANK, LOCAL), F32),
            pltpu.VMEM((2 * CHIPS, 8, RANK), F32),
            pltpu.VMEM((2 * CHIPS - 1, 8, RANK), F32),
            pltpu.VMEM((Z - 1, 8, RANK), F32),
            pltpu.VMEM((2 * CHIPS, 8, RANK), F32),
            pltpu.VMEM((RANK, RANK), F32),
            pltpu.VMEM((RANK, RANK), F32),
            pltpu.VMEM((BLOCKS, PLANE, 8, QUARTER), BF16),
            pltpu.VMEM((BLOCKS, PLANE - 1, 8, QUARTER), BF16),
            pltpu.VMEM((BLOCKS, PLANE, 8, QUARTER), BF16),
            pltpu.VMEM((BLOCKS, 2 * X, 8, TILE), F32),
            dma((3, PARTS)),
            dma((2,)),
            dma((2,)),
            dma((CHIPS,)),
            dma((CHIPS,)),
            dma((CHIPS,)),
            dma((CHIPS,)),
            dma((2,)),
            dma((2,)),
            dma((CHIPS,)),
            dma((CHIPS,)),
            dma((CHIPS,)),
            dma((CHIPS,)),
            dma((BLOCKS,)),
            dma((BLOCKS,)),
            dma((BLOCKS,)),
            dma((BLOCKS,)),
            dma((BLOCKS,)),
            dma((BLOCKS,)),
        ],
        compiler_params=pltpu.CompilerParams(
            collective_id=0, has_side_effects=True, vmem_limit_bytes=CORE_MIB * 1024 * 1024
        ),
    )(moment, change, factor)


def final_kernel(m_ref, g_ref, o_ref, r_ref, s_ref, nm_ref, sd_ref, nf_ref, fv):
    i = pl.program_id(0)

    @pl.when(i == 0)
    def _():
        fv[...] = (r_ref[...].astype(F32) * s_ref[:, 0:1]).astype(BF16)

    rows = pl.ds(pl.multiple_of(i * TILE, TILE), TILE)
    low = o_ref[rows, :]
    nm_ref[...] = m_ref[...].astype(F32) + g_ref[...].astype(F32) - 0.05 * low_dot(low, r_ref[...])
    sd_ref[...] = (jnp.sqrt(F32(ROWS / RANK)) * low_dot(low, fv[...])).astype(BF16)
    nf_ref[...] = (r_ref[:, rows].astype(F32) * s_ref[...]).T


def final(moment, change, ortho, right_t, scale):
    row = lambda i: (i, 0)
    vmem = pl.BlockSpec(memory_space=pltpu.VMEM)
    return pl.pallas_call(
        final_kernel,
        grid=(LOCAL // TILE,),
        out_shape=(
            jax.ShapeDtypeStruct((LOCAL, LOCAL), F32),
            jax.ShapeDtypeStruct((LOCAL, LOCAL), BF16),
            jax.ShapeDtypeStruct((LOCAL, RANK), F32),
        ),
        in_specs=[pl.BlockSpec((TILE, LOCAL), row), pl.BlockSpec((TILE, LOCAL), row), vmem, vmem, vmem],
        out_specs=(
            pl.BlockSpec((TILE, LOCAL), row),
            pl.BlockSpec((TILE, LOCAL), row),
            pl.BlockSpec((TILE, RANK), row),
        ),
        scratch_shapes=[pltpu.VMEM((RANK, LOCAL), BF16)],
        compiler_params=pltpu.CompilerParams(vmem_limit_bytes=FINAL_MIB * 1024 * 1024),
    )(moment, change, ortho, right_t, scale)


def local(momentum, gradient, factor):
    new_momentum, step_direction, new_factor = final(momentum[0], gradient[0], *core(momentum[0], gradient[0], factor))
    return new_momentum[None], step_direction, new_factor


def solution(mesh):
    in_specs = (P("dp", "fsdp", "tensor"), P("dp", "fsdp", "tensor"), P("tensor", None))
    out_specs = (P("dp", "fsdp", "tensor"), P("fsdp", "tensor"), P("tensor", None))
    return jax.shard_map(local, mesh=mesh, in_specs=in_specs, out_specs=out_specs, check_vma=False)
```

```python
import jax
import jax.numpy as jnp
from jax import lax
from jax.experimental import pallas as pl
from jax.experimental.pallas import tpu as pltpu
from jax.sharding import PartitionSpec as P

ROWS = 8192
COLS = 8192
RANK = 256

MESH = pl.DeviceIdType.MESH
HIGHEST = lax.Precision.HIGHEST
F32 = jnp.float32
BF16 = jnp.bfloat16
BLOCK = 64
BLOCKS = RANK // BLOCK
Y, Z, X = 4, 8, 4
STOP = 99
CORE_MIB = 52
FINAL_MIB = 24
CHIPS = X * Y
PLANE = Y * Z
LOCAL = 1024
HALF = LOCAL // 2
OWN = LOCAL // (2 * CHIPS)
PARTS = 4
CHUNK = LOCAL // PARTS
TILE = 128
WIDE = 256
QUARTER = LOCAL // Y


def dot(a, b):
    return jnp.dot(a, b, precision=HIGHEST, preferred_element_type=F32)


def low_dot(a, b):
    return jnp.dot(a, b, preferred_element_type=F32)


def factor_block(w, size):
    lanes = w.shape[1]
    row = lax.broadcasted_iota(jnp.int32, (8, lanes), 0)
    done = []
    for j in range(0, size, 8):
        v = w[0:8, :]
        p = [jnp.broadcast_to(v[m : m + 1, :], (8, lanes)) for m in range(8)]
        a = [
            [jnp.broadcast_to(p[i][:, j + m : j + m + 1], (8, lanes)) for m in range(i + 1)]
            for i in range(8)
        ]
        rest = w[8:, :]
        n = rest.shape[0]
        columns = [jnp.broadcast_to(rest[:, j + m : j + m + 1], (n, lanes)) for m in range(8)] if n else []
        low = [[None] * 8 for _ in range(8)]
        inverse = [None] * 8
        for k in range(8):
            inverse[k] = 1.0 / a[k][k]
            for i in range(k + 1, 8):
                low[i][k] = a[i][k] * inverse[k]
            for i in range(k + 1, 8):
                for m in range(k + 1, i + 1):
                    a[i][m] = a[i][m] - low[i][k] * a[m][k]
            for i in range(k + 1, 8):
                p[i] = p[i] - low[i][k] * p[k]
        out = p[7] * lax.rsqrt(a[7][7])
        for k in range(6, -1, -1):
            out = jnp.where(row == k, p[k] * lax.rsqrt(a[k][k]), out)
        done.append(out)
        if n:
            q = [None] * 8
            for k in range(7, -1, -1):
                q[k] = p[k] * inverse[k]
                for i in range(7, k, -1):
                    q[k] = q[k] - low[i][k] * q[i]
            for k in range(8):
                rest = rest - columns[k] * jnp.broadcast_to(q[k][0:1, :], (n, lanes))
            w = rest
    return jnp.concatenate(done, axis=0)


def eliminate(gram, inv, block):
    lo, hi = block * BLOCK, (block + 1) * BLOCK
    rows = gram[lo:hi, :]
    r_i = lax.broadcasted_iota(jnp.int32, (BLOCK, BLOCK), 0)
    c_i = lax.broadcasted_iota(jnp.int32, (BLOCK, BLOCK), 1)
    eye = jnp.where(r_i == c_i, 1.0, 0.0).astype(F32)
    root = factor_block(jnp.concatenate([rows[:, lo:hi], eye], axis=1), BLOCK)[:, BLOCK:]
    mine = dot(root, inv[lo:hi, :])
    inv[lo:hi, :] = mine
    if hi < RANK:
        upper = dot(root, rows)
        below = upper.T[hi:, :]
        gram[hi:, :] = gram[hi:, :] - dot(below, upper)
        inv[hi:, :] = inv[hi:, :] - dot(below, mine)
    return mine


def remote(src, dst, send, recv, **where):
    return pltpu.make_async_remote_copy(
        src_ref=src, dst_ref=dst, send_sem=send, recv_sem=recv, device_id=where, device_id_type=MESH
    )


def take(ref, sem):
    pltpu.make_async_copy(ref, ref, sem).wait()


def hops(step, size):
    return min(step, size - step)


def by_distance(*sizes):
    steps = [()]
    for size in sizes:
        steps = [s + (i,) for s in steps for i in range(size)]
    far = lambda s: sum(hops(a, n) for a, n in zip(s, sizes) if n > 2)
    return sorted([s for s in steps if any(s)], key=far, reverse=True)


CHIP_STEPS = by_distance(Y, X)
PLANE_STEPS = by_distance(Y, X, 2)
LINE_STEPS = by_distance(Y, Z)
Z_STEPS = by_distance(Z)
Y_STEPS = by_distance(Y)
X_STEPS = by_distance(X, 2)


def core_kernel(
    m_hbm, g_hbm, f_hbm,
    ortho, right_t, scale,
    mv, gv, sv, ff, fv, part, partner_in, half, outgoing, incoming, left, left_hi, left_lo, wide_t,
    gram, gram_in, line_in, gram_all, work, inv, rs_out, rs_in, y_in, y_sum, z_in, spread, square_in,
    load_sem, pair_sem, rs_sem, ag_send, ag_recv, fw_send, fw_recv, gr_sem,
    z_sem, gg_sem, r_send, r_recv, s_send, s_recv, n_send, n_recv, y_sem, z2_sem,
):
    y = lax.axis_index("dp")
    z = lax.axis_index("fsdp")
    t = lax.axis_index("tensor")
    x = t // 2
    c = lax.rem(t, 2)
    other = t + 1 - 2 * c
    me = c * CHIPS + y * X + x
    seat = y * Z + z
    own_base = c * HALF
    other_base = HALF - own_base

    def wrap(a, step, size):
        return lax.rem(a + step, size) if step else a

    barrier = pltpu.get_barrier_semaphore()

    def greet(**where):
        pl.semaphore_signal(barrier, inc=1, device_id=where, device_id_type=MESH)

    for dy, dz in LINE_STEPS:
        greet(dp=wrap(y, dy, Y), fsdp=wrap(z, dz, Z), tensor=t)
    for dy, dx, dc in PLANE_STEPS:
        greet(dp=wrap(y, dy, Y), fsdp=z, tensor=wrap(x, dx, X) * 2 + wrap(c, dc, 2))

    def first_row(i):
        base = other_base if i < PARTS // 2 else own_base
        return pl.multiple_of(base + (i % (PARTS // 2)) * CHUNK, CHUNK)

    def load(i, which):
        src, dst = ((m_hbm, mv), (g_hbm, gv))[which]
        rows = pl.ds(first_row(i), CHUNK)
        return pltpu.make_async_copy(src.at[rows, :], dst.at[rows, :], load_sem.at[which, i])

    load_factor = pltpu.make_async_copy(f_hbm, ff, load_sem.at[2, 0])
    load_factor.start()
    for i in range(PARTS):
        load(i, 0).start()
        load(i, 1).start()

    def chip_at(step, back=False):
        dy, dx = step
        if back:
            dy, dx = (Y - dy) % Y, (X - dx) % X
        return wrap(y, dy, Y), wrap(x, dx, X)

    pending = []

    def finish():
        for wait in pending:
            wait()

    load_factor.wait()
    fv[...] = ff[...].astype(BF16)
    for i in range(PARTS):
        load(i, 0).wait()
        load(i, 1).wait()
        rows = pl.ds(first_row(i), CHUNK)
        part[i * CHUNK : (i + 1) * CHUNK, :] = low_dot(mv[rows, :], fv[...]) + low_dot(gv[rows, :], fv[...])

    pl.semaphore_wait(barrier, len(LINE_STEPS) + len(PLANE_STEPS))
    if STOP == 1:
        return finish()
    to_partner = remote(part.at[0:HALF, :], partner_in, pair_sem.at[0], pair_sem.at[1], dp=y, fsdp=z, tensor=other)
    to_partner.start()
    pending.append(to_partner.wait_send)
    to_partner.wait_recv()
    both = (part[HALF:, :] + partner_in[...]).reshape(CHIPS, OWN, RANK)
    half[...] = both
    outgoing[...] = both.astype(BF16)

    for i, step in enumerate(CHIP_STEPS):
        py, px = chip_at(step)
        remote(outgoing.at[py * X + px], incoming.at[i], rs_sem.at[0], rs_sem.at[1], dp=py, fsdp=z, tensor=px * 2 + c).start()
    pending.append(lambda: take(incoming, rs_sem.at[0]))

    @pl.when(t >= 0)
    def _():
        sv[...] = (mv[...].astype(F32) + gv[...].astype(F32)).astype(BF16)

    take(incoming, rs_sem.at[1])
    if STOP == 2:
        return finish()
    mine = half[y * X + x]
    for i in range(CHIPS - 1):
        mine = mine + incoming[i].astype(F32)
    mine = mine * 0.25
    left[me] = mine

    gram[...] = dot(mine.T, mine).reshape(2 * CHIPS, 8, RANK)
    for i, (dy, dx, dc) in enumerate(PLANE_STEPS):
        py, px, pc = wrap(y, dy, Y), wrap(x, dx, X), wrap(c, dc, 2)
        remote(gram.at[pc * CHIPS + py * X + px], gram_in.at[i], gr_sem.at[0], gr_sem.at[1], dp=py, fsdp=z, tensor=px * 2 + pc).start()
    pending.append(lambda: take(gram_in, gr_sem.at[0]))

    def forward(ref, send, recv, i, step):
        py, px = chip_at(step, back=True)
        slot = c * CHIPS + py * X + px
        copy = remote(ref.at[slot], ref.at[slot], send.at[i], recv.at[i], dp=y, fsdp=z, tensor=other)
        copy.start()
        pending.append(copy.wait_send)
        return copy

    take(gram_in, gr_sem.at[1])
    mine = gram[me]
    for i in range(2 * CHIPS - 1):
        mine = mine + gram_in[i]
    gram[me] = mine

    for i, (dz,) in enumerate(Z_STEPS):
        remote(gram.at[me], line_in.at[i], z_sem.at[0], z_sem.at[1], dp=y, fsdp=wrap(z, dz, Z), tensor=t).start()
    pending.append(lambda: take(line_in, z_sem.at[0]))

    left_copies = []
    for i, step in enumerate(CHIP_STEPS):
        py, px = chip_at(step)
        copy = remote(left.at[me], left.at[me], ag_send.at[i], ag_recv.at[i], dp=py, fsdp=z, tensor=px * 2 + c)
        copy.start()
        left_copies.append(copy)
        pending.append(copy.wait_send)
    left_forwards = [forward(left, fw_send, fw_recv, CHIPS - 1, (0, 0))]

    take(line_in, z_sem.at[1])
    for i in range(Z - 1):
        mine = mine + line_in[i]
    gram_all[me] = mine

    slot = gram_all.at[me]
    for dy, dx, dc in PLANE_STEPS:
        remote(slot, slot, gg_sem.at[0], gg_sem.at[1], dp=wrap(y, dy, Y), fsdp=z, tensor=wrap(x, dx, X) * 2 + wrap(c, dc, 2)).start()
    pending.append(lambda: take(gram_in, gg_sem.at[0]))

    for i in range(CHIPS - 2, -1, -1):
        left_copies[i].wait_recv()
        left_forwards.append(forward(left, fw_send, fw_recv, i, CHIP_STEPS[i]))
    for copy in left_forwards:
        copy.wait_recv()

    @pl.when(t >= 0)
    def _():
        flat = left[...].reshape(LOCAL, RANK).T
        left_hi[...] = flat.astype(BF16)
        left_lo[...] = (flat - flat.astype(BF16).astype(F32)).astype(BF16)

    take(gram_in, gg_sem.at[1])
    if STOP == 5:
        return finish()
    work[...] = gram_all[...].reshape(RANK, RANK)
    r_i = lax.broadcasted_iota(jnp.int32, (RANK, RANK), 0)
    c_i = lax.broadcasted_iota(jnp.int32, (RANK, RANK), 1)
    inv[...] = jnp.where(r_i == c_i, 1.0, 0.0).astype(F32)

    last = BLOCKS - 1

    def send_right(b):
        if b == last:
            for i, (dy, dz) in enumerate(LINE_STEPS):
                py, pz = wrap(y, dy, Y), wrap(z, dz, Z)
                remote(rs_out.at[b, py * Z + pz], rs_in.at[i], r_send.at[b], r_recv.at[b], dp=py, fsdp=pz, tensor=t).start()
            pending.append(lambda: take(rs_in, r_send.at[b]))
            return
        for i, (dy,) in enumerate(Y_STEPS):
            py = wrap(y, dy, Y)
            remote(rs_out.at[b, pl.ds(py * Z, Z)], y_in.at[b, i], r_send.at[b], r_recv.at[b], dp=py, fsdp=z, tensor=t).start()
        pending.append(lambda: take(y_in.at[b], r_send.at[b]))

    def sum_y(b):
        take(y_in.at[b], r_recv.at[b])
        sums = rs_out[b, pl.ds(y * Z, Z)].astype(F32)
        for i in range(Y - 1):
            sums = sums + y_in[b, i].astype(F32)
        y_sum[b] = sums.astype(BF16)
        for i, (dz,) in enumerate(Z_STEPS):
            pz = wrap(z, dz, Z)
            remote(y_sum.at[b, pz], z_in.at[b, i], z2_sem.at[0, b], z2_sem.at[1, b], dp=y, fsdp=pz, tensor=t).start()
        pending.append(lambda: take(z_in.at[b], z2_sem.at[0, b]))

    def sum_z(b):
        slot = spread.at[b, seat]
        if b == last:
            take(rs_in, r_recv.at[b])
            mine = rs_out[b, seat].astype(F32)
            for i in range(PLANE - 1):
                mine = mine + rs_in[i].astype(F32)
            spread[b, seat] = (mine * 0.25).astype(BF16)
            for dy, dz in LINE_STEPS:
                remote(slot, slot, s_send.at[b], s_recv.at[b], dp=wrap(y, dy, Y), fsdp=wrap(z, dz, Z), tensor=t).start()
            pending.append(lambda: take(rs_in, s_send.at[b]))
            return
        take(z_in.at[b], z2_sem.at[1, b])
        mine = y_sum[b, z].astype(F32)
        for i in range(Z - 1):
            mine = mine + z_in[b, i].astype(F32)
        spread[b, seat] = (mine * 0.25).astype(BF16)
        for (dz,) in Z_STEPS:
            remote(slot, slot, s_send.at[b], s_recv.at[b], dp=y, fsdp=wrap(z, dz, Z), tensor=t).start()
        pending.append(lambda: take(z_in.at[b], s_send.at[b]))

    def spread_y(b):
        take(z_in.at[b], s_recv.at[b])
        line = spread.at[b, pl.ds(y * Z, Z)]
        for (dy,) in Y_STEPS:
            remote(line, line, y_sem.at[0, b], y_sem.at[1, b], dp=wrap(y, dy, Y), fsdp=z, tensor=t).start()
        pending.append(lambda: take(y_in.at[b], y_sem.at[0, b]))

    k_i = lax.broadcasted_iota(jnp.int32, (BLOCK, TILE), 0)
    l_i = lax.broadcasted_iota(jnp.int32, (BLOCK, TILE), 1)

    def collect(b):
        if b == last:
            take(rs_in, s_recv.at[b])
        else:
            take(y_in.at[b], y_sem.at[1, b])
        squares = jnp.zeros((BLOCK, QUARTER), F32)
        for py in range(Y):
            piece = jnp.concatenate([spread[b, py * Z + pz].astype(F32) for pz in range(Z)], axis=0)
            right_t[b * BLOCK : (b + 1) * BLOCK, py * QUARTER : (py + 1) * QUARTER] = piece.astype(BF16)
            squares = squares + piece * piece
        column = jnp.sum(squares, axis=1, keepdims=True)
        line = jnp.sum(jnp.where(k_i == l_i, column, 0.0), axis=0, keepdims=True)
        square_in[b, t] = jnp.broadcast_to(line, (8, TILE))
        for dx, dc in X_STEPS:
            slot = square_in.at[b, t]
            remote(slot, slot, n_send.at[b], n_recv.at[b], dp=y, fsdp=z, tensor=wrap(x, dx, X) * 2 + wrap(c, dc, 2)).start()
        pending.append(lambda: take(square_in.at[b, 1:], n_send.at[b]))

    def norm(b):
        take(square_in.at[b, 1:], n_recv.at[b])
        sums = square_in[b, 0]
        for i in range(1, 2 * X):
            sums = sums + square_in[b, i]
        column = jnp.sum(jnp.where(k_i == l_i, sums[0:1, :], 0.0), axis=1, keepdims=True)
        scale[b * BLOCK : (b + 1) * BLOCK, :] = jnp.broadcast_to(lax.rsqrt(column * (1.0 / COLS) + 1e-06), (BLOCK, TILE))

    def compute(b):
        rows_of = eliminate(work, inv, b)
        first = rows_of.astype(BF16)
        second = (rows_of - first.astype(F32)).astype(BF16)
        twice = low_dot(jnp.concatenate([first, second], axis=0), left_hi[...])
        wide = twice[:BLOCK] + twice[BLOCK:] + low_dot(first, left_lo[...])
        low = wide.astype(BF16)
        wide_t[b * BLOCK : (b + 1) * BLOCK, :] = wide
        term = low_dot(low, sv[...])
        for pz in range(Z):
            for py in range(Y):
                rs_out[b, py * Z + pz] = term[pz * 8 : pz * 8 + 8, py * QUARTER : (py + 1) * QUARTER].astype(BF16)

    for b in range(BLOCKS):
        pl.when(t >= 0)(lambda b=b: compute(b))
        send_right(b)
        if b >= 1:
            sum_y(b - 1)
        if b >= 2:
            sum_z(b - 2)
        if b >= 3:
            spread_y(b - 3)

    @pl.when(t >= 0)
    def _():
        ortho[...] = wide_t[...].T.astype(BF16)

    sum_z(last - 1)
    spread_y(last - 2)
    collect(0)
    sum_z(last)
    spread_y(last - 1)
    collect(1)
    collect(2)
    norm(0)
    norm(1)
    collect(last)
    norm(2)
    norm(last)
    finish()


def core(moment, change, factor):
    vmem = pl.BlockSpec(memory_space=pltpu.VMEM)
    hbm = pl.BlockSpec(memory_space=pltpu.HBM)
    dma = pltpu.SemaphoreType.DMA
    return pl.pallas_call(
        core_kernel,
        out_shape=(
            jax.ShapeDtypeStruct((LOCAL, RANK), BF16),
            jax.ShapeDtypeStruct((RANK, LOCAL), BF16),
            jax.ShapeDtypeStruct((RANK, TILE), F32),
        ),
        in_specs=[hbm, hbm, hbm],
        out_specs=(vmem, vmem, vmem),
        scratch_shapes=[
            pltpu.VMEM((LOCAL, LOCAL), BF16),
            pltpu.VMEM((LOCAL, LOCAL), BF16),
            pltpu.VMEM((LOCAL, LOCAL), BF16),
            pltpu.VMEM((LOCAL, RANK), F32),
            pltpu.VMEM((LOCAL, RANK), BF16),
            pltpu.VMEM((LOCAL, RANK), F32),
            pltpu.VMEM((HALF, RANK), F32),
            pltpu.VMEM((CHIPS, OWN, RANK), F32),
            pltpu.VMEM((CHIPS, OWN, RANK), BF16),
            pltpu.VMEM((CHIPS - 1, OWN, RANK), BF16),
            pltpu.VMEM((2 * CHIPS, OWN, RANK), F32),
            pltpu.VMEM((RANK, LOCAL), BF16),
            pltpu.VMEM((RANK, LOCAL), BF16),
            pltpu.VMEM((RANK, LOCAL), F32),
            pltpu.VMEM((2 * CHIPS, 8, RANK), F32),
            pltpu.VMEM((2 * CHIPS - 1, 8, RANK), F32),
            pltpu.VMEM((Z - 1, 8, RANK), F32),
            pltpu.VMEM((2 * CHIPS, 8, RANK), F32),
            pltpu.VMEM((RANK, RANK), F32),
            pltpu.VMEM((RANK, RANK), F32),
            pltpu.VMEM((BLOCKS, PLANE, 8, QUARTER), BF16),
            pltpu.VMEM((PLANE - 1, 8, QUARTER), BF16),
            pltpu.VMEM((BLOCKS - 1, Y - 1, Z, 8, QUARTER), BF16),
            pltpu.VMEM((BLOCKS - 1, Z, 8, QUARTER), BF16),
            pltpu.VMEM((BLOCKS - 1, Z - 1, 8, QUARTER), BF16),
            pltpu.VMEM((BLOCKS, PLANE, 8, QUARTER), BF16),
            pltpu.VMEM((BLOCKS, 2 * X, 8, TILE), F32),
            dma((3, PARTS)),
            dma((2,)),
            dma((2,)),
            dma((CHIPS,)),
            dma((CHIPS,)),
            dma((CHIPS,)),
            dma((CHIPS,)),
            dma((2,)),
            dma((2,)),
            dma((2,)),
            dma((BLOCKS,)),
            dma((BLOCKS,)),
            dma((BLOCKS,)),
            dma((BLOCKS,)),
            dma((BLOCKS,)),
            dma((BLOCKS,)),
            dma((2, BLOCKS)),
            dma((2, BLOCKS)),
        ],
        compiler_params=pltpu.CompilerParams(
            collective_id=0, has_side_effects=True, vmem_limit_bytes=CORE_MIB * 1024 * 1024
        ),
    )(moment, change, factor)


def final_kernel(m_ref, g_ref, o_ref, r_ref, s_ref, nm_ref, sd_ref, nf_ref):
    right = r_ref[...]
    factor_next = right.astype(F32) * s_ref[:, 0:1]
    nm_ref[...] = m_ref[...].astype(F32) + g_ref[...].astype(F32) - 0.05 * low_dot(o_ref[...], right)
    step = low_dot(o_ref[...], factor_next.astype(BF16))
    sd_ref[...] = (jnp.sqrt(F32(ROWS / RANK)) * step).astype(BF16)
    nf_ref[...] = factor_next.T


def final(moment, change, ortho, right_t, scale):
    col = lambda i: (0, i)
    vmem = pl.BlockSpec(memory_space=pltpu.VMEM)
    return pl.pallas_call(
        final_kernel,
        grid=(LOCAL // WIDE,),
        out_shape=(
            jax.ShapeDtypeStruct((LOCAL, LOCAL), F32),
            jax.ShapeDtypeStruct((LOCAL, LOCAL), BF16),
            jax.ShapeDtypeStruct((LOCAL, RANK), F32),
        ),
        in_specs=[
            pl.BlockSpec((LOCAL, WIDE), col),
            pl.BlockSpec((LOCAL, WIDE), col),
            vmem,
            pl.BlockSpec((RANK, WIDE), col),
            vmem,
        ],
        out_specs=(
            pl.BlockSpec((LOCAL, WIDE), col),
            pl.BlockSpec((LOCAL, WIDE), col),
            pl.BlockSpec((WIDE, RANK), lambda i: (i, 0)),
        ),
        compiler_params=pltpu.CompilerParams(vmem_limit_bytes=FINAL_MIB * 1024 * 1024),
    )(moment, change, ortho, right_t, scale)


def local(momentum, gradient, factor):
    new_momentum, step_direction, new_factor = final(momentum[0], gradient[0], *core(momentum[0], gradient[0], factor))
    return new_momentum[None], step_direction, new_factor


def solution(mesh):
    in_specs = (P("dp", "fsdp", "tensor"), P("dp", "fsdp", "tensor"), P("tensor", None))
    out_specs = (P("dp", "fsdp", "tensor"), P("fsdp", "tensor"), P("tensor", None))
    return jax.shard_map(local, mesh=mesh, in_specs=in_specs, out_specs=out_specs, check_vma=False)
```

```python
import jax
import jax.numpy as jnp
from jax import lax
from jax.experimental import pallas as pl
from jax.experimental.pallas import tpu as pltpu
from jax.sharding import PartitionSpec as P

ROWS = 8192
COLS = 8192
RANK = 256

MESH = pl.DeviceIdType.MESH
HIGHEST = lax.Precision.HIGHEST
F32 = jnp.float32
BF16 = jnp.bfloat16
BLOCK = 64
BLOCKS = RANK // BLOCK
Y, Z, X = 4, 8, 4
STOP = 99
CORE_MIB = 52
FINAL_MIB = 24
CHIPS = X * Y
PLANE = Y * Z
LOCAL = 1024
HALF = LOCAL // 2
OWN = LOCAL // (2 * CHIPS)
PARTS = 4
CHUNK = LOCAL // PARTS
TILE = 128
WIDE = 512
QUARTER = LOCAL // Y


def dot(a, b):
    return jnp.dot(a, b, precision=HIGHEST, preferred_element_type=F32)


def low_dot(a, b):
    return jnp.dot(a, b, preferred_element_type=F32)


def factor_block(w, size):
    lanes = w.shape[1]
    row = lax.broadcasted_iota(jnp.int32, (8, lanes), 0)
    done = []
    for j in range(0, size, 8):
        v = w[0:8, :]
        p = [jnp.broadcast_to(v[m : m + 1, :], (8, lanes)) for m in range(8)]
        a = [
            [jnp.broadcast_to(p[i][:, j + m : j + m + 1], (8, lanes)) for m in range(i + 1)]
            for i in range(8)
        ]
        rest = w[8:, :]
        n = rest.shape[0]
        columns = [jnp.broadcast_to(rest[:, j + m : j + m + 1], (n, lanes)) for m in range(8)] if n else []
        low = [[None] * 8 for _ in range(8)]
        inverse = [None] * 8
        for k in range(8):
            inverse[k] = 1.0 / a[k][k]
            for i in range(k + 1, 8):
                low[i][k] = a[i][k] * inverse[k]
            for i in range(k + 1, 8):
                for m in range(k + 1, i + 1):
                    a[i][m] = a[i][m] - low[i][k] * a[m][k]
            for i in range(k + 1, 8):
                p[i] = p[i] - low[i][k] * p[k]
        out = p[7] * lax.rsqrt(a[7][7])
        for k in range(6, -1, -1):
            out = jnp.where(row == k, p[k] * lax.rsqrt(a[k][k]), out)
        done.append(out)
        if n:
            q = [None] * 8
            for k in range(7, -1, -1):
                q[k] = p[k] * inverse[k]
                for i in range(7, k, -1):
                    q[k] = q[k] - low[i][k] * q[i]
            for k in range(8):
                rest = rest - columns[k] * jnp.broadcast_to(q[k][0:1, :], (n, lanes))
            w = rest
    return jnp.concatenate(done, axis=0)


def eliminate(gram, inv, block):
    lo, hi = block * BLOCK, (block + 1) * BLOCK
    rows = gram[lo:hi, :]
    r_i = lax.broadcasted_iota(jnp.int32, (BLOCK, BLOCK), 0)
    c_i = lax.broadcasted_iota(jnp.int32, (BLOCK, BLOCK), 1)
    eye = jnp.where(r_i == c_i, 1.0, 0.0).astype(F32)
    root = factor_block(jnp.concatenate([rows[:, lo:hi], eye], axis=1), BLOCK)[:, BLOCK:]
    mine = dot(root, inv[lo:hi, :])
    inv[lo:hi, :] = mine
    if hi < RANK:
        upper = dot(root, rows)
        below = upper.T[hi:, :]
        gram[hi:, :] = gram[hi:, :] - dot(below, upper)
        inv[hi:, :] = inv[hi:, :] - dot(below, mine)
    return mine


def remote(src, dst, send, recv, **where):
    return pltpu.make_async_remote_copy(
        src_ref=src, dst_ref=dst, send_sem=send, recv_sem=recv, device_id=where, device_id_type=MESH
    )


def take(ref, sem):
    pltpu.make_async_copy(ref, ref, sem).wait()


def hops(step, size):
    return min(step, size - step)


def by_distance(*sizes):
    steps = [()]
    for size in sizes:
        steps = [s + (i,) for s in steps for i in range(size)]
    far = lambda s: sum(hops(a, n) for a, n in zip(s, sizes) if n > 2)
    return sorted([s for s in steps if any(s)], key=far, reverse=True)


CHIP_STEPS = by_distance(Y, X)
PLANE_STEPS = by_distance(Y, X, 2)
LINE_STEPS = by_distance(Y, Z)
Z_STEPS = by_distance(Z)
Y_STEPS = by_distance(Y)
X_STEPS = by_distance(X, 2)


def core_kernel(
    m_hbm, g_hbm, f_hbm,
    ortho, right_t, scale,
    mv, gv, sv, ff, fv, part, partner_out, partner_in, half, outgoing, incoming, left, left_hi, left_lo, wide_t,
    gram, gram_in, line_in, gram_all, work, inv, rs_out, rs_in, y_in, y_sum, z_in, spread, square_in,
    load_sem, pair_sem, rs_sem, ag_send, ag_recv, fw_send, fw_recv, gr_sem,
    z_sem, gg_sem, r_send, r_recv, s_send, s_recv, n_send, n_recv, y_sem, z2_sem,
):
    y = lax.axis_index("dp")
    z = lax.axis_index("fsdp")
    t = lax.axis_index("tensor")
    x = t // 2
    c = lax.rem(t, 2)
    other = t + 1 - 2 * c
    me = c * CHIPS + y * X + x
    seat = y * Z + z
    own_base = c * HALF
    other_base = HALF - own_base

    def wrap(a, step, size):
        return lax.rem(a + step, size) if step else a

    barrier = pltpu.get_barrier_semaphore()

    def greet(**where):
        pl.semaphore_signal(barrier, inc=1, device_id=where, device_id_type=MESH)

    for dy, dx, dc in PLANE_STEPS:
        greet(dp=wrap(y, dy, Y), fsdp=z, tensor=wrap(x, dx, X) * 2 + wrap(c, dc, 2))
    for (dz,) in Z_STEPS:
        greet(dp=y, fsdp=wrap(z, dz, Z), tensor=t)

    def first_row(i):
        base = other_base if i < PARTS // 2 else own_base
        return pl.multiple_of(base + (i % (PARTS // 2)) * CHUNK, CHUNK)

    def load(i, which):
        src, dst = ((m_hbm, mv), (g_hbm, gv))[which]
        rows = pl.ds(first_row(i), CHUNK)
        return pltpu.make_async_copy(src.at[rows, :], dst.at[rows, :], load_sem.at[which, i])

    load_factor = pltpu.make_async_copy(f_hbm, ff, load_sem.at[2, 0])
    load_factor.start()
    for i in range(PARTS):
        load(i, 0).start()
        load(i, 1).start()

    def chip_at(step, back=False):
        dy, dx = step
        if back:
            dy, dx = (Y - dy) % Y, (X - dx) % X
        return wrap(y, dy, Y), wrap(x, dx, X)

    pending = []

    def finish():
        for wait in pending:
            wait()

    load_factor.wait()
    fv[...] = ff[...].astype(BF16)
    for i in range(PARTS):
        load(i, 0).wait()
        load(i, 1).wait()
        rows = pl.ds(first_row(i), CHUNK)
        product = low_dot(mv[rows, :], fv[...]) + low_dot(gv[rows, :], fv[...])
        if i < PARTS // 2:
            partner_out[i * CHUNK : (i + 1) * CHUNK, :] = product.astype(BF16)
        else:
            part[i * CHUNK - HALF : (i + 1) * CHUNK - HALF, :] = product

    pl.semaphore_wait(barrier, len(Z_STEPS) + len(PLANE_STEPS))
    if STOP == 1:
        return finish()
    to_partner = remote(partner_out, partner_in, pair_sem.at[0], pair_sem.at[1], dp=y, fsdp=z, tensor=other)
    to_partner.start()
    pending.append(to_partner.wait_send)
    to_partner.wait_recv()
    both = (part[...] + partner_in[...].astype(F32)).reshape(CHIPS, OWN, RANK)
    half[...] = both
    outgoing[...] = both.astype(BF16)

    for i, step in enumerate(CHIP_STEPS):
        py, px = chip_at(step)
        remote(outgoing.at[py * X + px], incoming.at[i], rs_sem.at[0], rs_sem.at[1], dp=py, fsdp=z, tensor=px * 2 + c).start()
    pending.append(lambda: take(incoming, rs_sem.at[0]))

    @pl.when(t >= 0)
    def _():
        sv[...] = (mv[...].astype(F32) + gv[...].astype(F32)).astype(BF16)

    take(incoming, rs_sem.at[1])
    if STOP == 2:
        return finish()
    mine = half[y * X + x]
    for i in range(CHIPS - 1):
        mine = mine + incoming[i].astype(F32)
    mine = mine * 0.25
    left[me] = mine

    gram[...] = dot(mine.T, mine).reshape(2 * CHIPS, 8, RANK)
    for i, (dy, dx, dc) in enumerate(PLANE_STEPS):
        py, px, pc = wrap(y, dy, Y), wrap(x, dx, X), wrap(c, dc, 2)
        remote(gram.at[pc * CHIPS + py * X + px], gram_in.at[i], gr_sem.at[0], gr_sem.at[1], dp=py, fsdp=z, tensor=px * 2 + pc).start()
    pending.append(lambda: take(gram_in, gr_sem.at[0]))

    def forward(ref, send, recv, i, step):
        py, px = chip_at(step, back=True)
        slot = c * CHIPS + py * X + px
        copy = remote(ref.at[slot], ref.at[slot], send.at[i], recv.at[i], dp=y, fsdp=z, tensor=other)
        copy.start()
        pending.append(copy.wait_send)
        return copy

    take(gram_in, gr_sem.at[1])
    mine = gram[me]
    for i in range(2 * CHIPS - 1):
        mine = mine + gram_in[i]
    gram[me] = mine

    for i, (dz,) in enumerate(Z_STEPS):
        remote(gram.at[me], line_in.at[i], z_sem.at[0], z_sem.at[1], dp=y, fsdp=wrap(z, dz, Z), tensor=t).start()
    pending.append(lambda: take(line_in, z_sem.at[0]))

    left_copies = []
    for i, step in enumerate(CHIP_STEPS):
        py, px = chip_at(step)
        copy = remote(left.at[me], left.at[me], ag_send.at[i], ag_recv.at[i], dp=py, fsdp=z, tensor=px * 2 + c)
        copy.start()
        left_copies.append(copy)
        pending.append(copy.wait_send)
    left_forwards = [forward(left, fw_send, fw_recv, CHIPS - 1, (0, 0))]

    take(line_in, z_sem.at[1])
    for i in range(Z - 1):
        mine = mine + line_in[i]
    gram_all[me] = mine

    slot = gram_all.at[me]
    for dy, dx, dc in PLANE_STEPS:
        remote(slot, slot, gg_sem.at[0], gg_sem.at[1], dp=wrap(y, dy, Y), fsdp=z, tensor=wrap(x, dx, X) * 2 + wrap(c, dc, 2)).start()
    pending.append(lambda: take(gram_in, gg_sem.at[0]))

    for i in range(CHIPS - 2, -1, -1):
        left_copies[i].wait_recv()
        left_forwards.append(forward(left, fw_send, fw_recv, i, CHIP_STEPS[i]))
    for copy in left_forwards:
        copy.wait_recv()

    @pl.when(t >= 0)
    def _():
        flat = left[...].reshape(LOCAL, RANK).T
        left_hi[...] = flat.astype(BF16)
        left_lo[...] = (flat - flat.astype(BF16).astype(F32)).astype(BF16)

    take(gram_in, gg_sem.at[1])
    if STOP == 5:
        return finish()
    work[...] = gram_all[...].reshape(RANK, RANK)
    r_i = lax.broadcasted_iota(jnp.int32, (RANK, RANK), 0)
    c_i = lax.broadcasted_iota(jnp.int32, (RANK, RANK), 1)
    inv[...] = jnp.where(r_i == c_i, 1.0, 0.0).astype(F32)

    last = BLOCKS - 1

    def send_right(b):
        if b == last:
            for i, (dy, dz) in enumerate(LINE_STEPS):
                py, pz = wrap(y, dy, Y), wrap(z, dz, Z)
                remote(rs_out.at[b, py * Z + pz], rs_in.at[i], r_send.at[b], r_recv.at[b], dp=py, fsdp=pz, tensor=t).start()
            pending.append(lambda: take(rs_in, r_send.at[b]))
            return
        for i, (dy,) in enumerate(Y_STEPS):
            py = wrap(y, dy, Y)
            remote(rs_out.at[b, pl.ds(py * Z, Z)], y_in.at[b, i], r_send.at[b], r_recv.at[b], dp=py, fsdp=z, tensor=t).start()
        pending.append(lambda: take(y_in.at[b], r_send.at[b]))

    def sum_y(b):
        take(y_in.at[b], r_recv.at[b])
        sums = rs_out[b, pl.ds(y * Z, Z)].astype(F32)
        for i in range(Y - 1):
            sums = sums + y_in[b, i].astype(F32)
        y_sum[b] = sums.astype(BF16)
        for i, (dz,) in enumerate(Z_STEPS):
            pz = wrap(z, dz, Z)
            remote(y_sum.at[b, pz], z_in.at[b, i], z2_sem.at[0, b], z2_sem.at[1, b], dp=y, fsdp=pz, tensor=t).start()
        pending.append(lambda: take(z_in.at[b], z2_sem.at[0, b]))

    def sum_z(b):
        slot = spread.at[b, seat]
        if b == last:
            take(rs_in, r_recv.at[b])
            mine = rs_out[b, seat].astype(F32)
            for i in range(PLANE - 1):
                mine = mine + rs_in[i].astype(F32)
            spread[b, seat] = (mine * 0.25).astype(BF16)
            for dy, dz in LINE_STEPS:
                remote(slot, slot, s_send.at[b], s_recv.at[b], dp=wrap(y, dy, Y), fsdp=wrap(z, dz, Z), tensor=t).start()
            pending.append(lambda: take(rs_in, s_send.at[b]))
            return
        take(z_in.at[b], z2_sem.at[1, b])
        mine = y_sum[b, z].astype(F32)
        for i in range(Z - 1):
            mine = mine + z_in[b, i].astype(F32)
        spread[b, seat] = (mine * 0.25).astype(BF16)
        for (dz,) in Z_STEPS:
            remote(slot, slot, s_send.at[b], s_recv.at[b], dp=y, fsdp=wrap(z, dz, Z), tensor=t).start()
        pending.append(lambda: take(z_in.at[b], s_send.at[b]))

    def spread_y(b):
        take(z_in.at[b], s_recv.at[b])
        line = spread.at[b, pl.ds(y * Z, Z)]
        for (dy,) in Y_STEPS:
            remote(line, line, y_sem.at[0, b], y_sem.at[1, b], dp=wrap(y, dy, Y), fsdp=z, tensor=t).start()
        pending.append(lambda: take(y_in.at[b], y_sem.at[0, b]))

    k_i = lax.broadcasted_iota(jnp.int32, (BLOCK, TILE), 0)
    l_i = lax.broadcasted_iota(jnp.int32, (BLOCK, TILE), 1)

    def collect(b):
        if b == last:
            take(rs_in, s_recv.at[b])
        else:
            take(y_in.at[b], y_sem.at[1, b])
        squares = jnp.zeros((BLOCK, QUARTER), F32)
        for py in range(Y):
            piece = jnp.concatenate([spread[b, py * Z + pz].astype(F32) for pz in range(Z)], axis=0)
            right_t[b * BLOCK : (b + 1) * BLOCK, py * QUARTER : (py + 1) * QUARTER] = piece.astype(BF16)
            squares = squares + piece * piece
        column = jnp.sum(squares, axis=1, keepdims=True)
        line = jnp.sum(jnp.where(k_i == l_i, column, 0.0), axis=0, keepdims=True)
        square_in[b, t] = jnp.broadcast_to(line, (8, TILE))
        for dx, dc in X_STEPS:
            slot = square_in.at[b, t]
            remote(slot, slot, n_send.at[b], n_recv.at[b], dp=y, fsdp=z, tensor=wrap(x, dx, X) * 2 + wrap(c, dc, 2)).start()
        pending.append(lambda: take(square_in.at[b, 1:], n_send.at[b]))

    def norm(b):
        take(square_in.at[b, 1:], n_recv.at[b])
        sums = square_in[b, 0]
        for i in range(1, 2 * X):
            sums = sums + square_in[b, i]
        column = jnp.sum(jnp.where(k_i == l_i, sums[0:1, :], 0.0), axis=1, keepdims=True)
        scale[b * BLOCK : (b + 1) * BLOCK, :] = jnp.broadcast_to(lax.rsqrt(column * (1.0 / COLS) + 1e-06), (BLOCK, TILE))

    def compute(b):
        rows_of = eliminate(work, inv, b)
        first = rows_of.astype(BF16)
        second = (rows_of - first.astype(F32)).astype(BF16)
        twice = low_dot(jnp.concatenate([first, second], axis=0), left_hi[...])
        wide = twice[:BLOCK] + twice[BLOCK:] + low_dot(first, left_lo[...])
        low = wide.astype(BF16)
        wide_t[b * BLOCK : (b + 1) * BLOCK, :] = wide
        term = low_dot(low, sv[...])
        for pz in range(Z):
            for py in range(Y):
                rs_out[b, py * Z + pz] = term[pz * 8 : pz * 8 + 8, py * QUARTER : (py + 1) * QUARTER].astype(BF16)

    for b in range(BLOCKS):
        pl.when(t >= 0)(lambda b=b: compute(b))
        send_right(b)
        if b >= 1:
            sum_y(b - 1)
        if b >= 2:
            sum_z(b - 2)
        if b >= 3:
            spread_y(b - 3)

    @pl.when(t >= 0)
    def _():
        ortho[...] = wide_t[...].T.astype(BF16)

    sum_z(last - 1)
    spread_y(last - 2)
    collect(0)
    sum_z(last)
    spread_y(last - 1)
    collect(1)
    collect(2)
    norm(0)
    norm(1)
    collect(last)
    norm(2)
    norm(last)
    finish()


def core(moment, change, factor):
    vmem = pl.BlockSpec(memory_space=pltpu.VMEM)
    hbm = pl.BlockSpec(memory_space=pltpu.HBM)
    dma = pltpu.SemaphoreType.DMA
    return pl.pallas_call(
        core_kernel,
        out_shape=(
            jax.ShapeDtypeStruct((LOCAL, RANK), BF16),
            jax.ShapeDtypeStruct((RANK, LOCAL), BF16),
            jax.ShapeDtypeStruct((RANK, TILE), F32),
        ),
        in_specs=[hbm, hbm, hbm],
        out_specs=(vmem, vmem, vmem),
        scratch_shapes=[
            pltpu.VMEM((LOCAL, LOCAL), BF16),
            pltpu.VMEM((LOCAL, LOCAL), BF16),
            pltpu.VMEM((LOCAL, LOCAL), BF16),
            pltpu.VMEM((LOCAL, RANK), F32),
            pltpu.VMEM((LOCAL, RANK), BF16),
            pltpu.VMEM((HALF, RANK), F32),
            pltpu.VMEM((HALF, RANK), BF16),
            pltpu.VMEM((HALF, RANK), BF16),
            pltpu.VMEM((CHIPS, OWN, RANK), F32),
            pltpu.VMEM((CHIPS, OWN, RANK), BF16),
            pltpu.VMEM((CHIPS - 1, OWN, RANK), BF16),
            pltpu.VMEM((2 * CHIPS, OWN, RANK), F32),
            pltpu.VMEM((RANK, LOCAL), BF16),
            pltpu.VMEM((RANK, LOCAL), BF16),
            pltpu.VMEM((RANK, LOCAL), F32),
            pltpu.VMEM((2 * CHIPS, 8, RANK), F32),
            pltpu.VMEM((2 * CHIPS - 1, 8, RANK), F32),
            pltpu.VMEM((Z - 1, 8, RANK), F32),
            pltpu.VMEM((2 * CHIPS, 8, RANK), F32),
            pltpu.VMEM((RANK, RANK), F32),
            pltpu.VMEM((RANK, RANK), F32),
            pltpu.VMEM((BLOCKS, PLANE, 8, QUARTER), BF16),
            pltpu.VMEM((PLANE - 1, 8, QUARTER), BF16),
            pltpu.VMEM((BLOCKS - 1, Y - 1, Z, 8, QUARTER), BF16),
            pltpu.VMEM((BLOCKS - 1, Z, 8, QUARTER), BF16),
            pltpu.VMEM((BLOCKS - 1, Z - 1, 8, QUARTER), BF16),
            pltpu.VMEM((BLOCKS, PLANE, 8, QUARTER), BF16),
            pltpu.VMEM((BLOCKS, 2 * X, 8, TILE), F32),
            dma((3, PARTS)),
            dma((2,)),
            dma((2,)),
            dma((CHIPS,)),
            dma((CHIPS,)),
            dma((CHIPS,)),
            dma((CHIPS,)),
            dma((2,)),
            dma((2,)),
            dma((2,)),
            dma((BLOCKS,)),
            dma((BLOCKS,)),
            dma((BLOCKS,)),
            dma((BLOCKS,)),
            dma((BLOCKS,)),
            dma((BLOCKS,)),
            dma((2, BLOCKS)),
            dma((2, BLOCKS)),
        ],
        compiler_params=pltpu.CompilerParams(
            collective_id=0, has_side_effects=True, vmem_limit_bytes=CORE_MIB * 1024 * 1024
        ),
    )(moment, change, factor)


def final_kernel(m_ref, g_ref, o_ref, r_ref, s_ref, nm_ref, sd_ref, nf_ref):
    right = r_ref[...]
    factor_next = right.astype(F32) * s_ref[:, 0:1]
    nm_ref[...] = m_ref[...].astype(F32) + g_ref[...].astype(F32) - 0.05 * low_dot(o_ref[...], right)
    step = low_dot(o_ref[...], factor_next.astype(BF16))
    sd_ref[...] = (jnp.sqrt(F32(ROWS / RANK)) * step).astype(BF16)
    nf_ref[...] = factor_next.T


def final(moment, change, ortho, right_t, scale):
    col = lambda i: (0, i)
    vmem = pl.BlockSpec(memory_space=pltpu.VMEM)
    return pl.pallas_call(
        final_kernel,
        grid=(LOCAL // WIDE,),
        out_shape=(
            jax.ShapeDtypeStruct((LOCAL, LOCAL), F32),
            jax.ShapeDtypeStruct((LOCAL, LOCAL), BF16),
            jax.ShapeDtypeStruct((LOCAL, RANK), F32),
        ),
        in_specs=[
            pl.BlockSpec((LOCAL, WIDE), col),
            pl.BlockSpec((LOCAL, WIDE), col),
            vmem,
            pl.BlockSpec((RANK, WIDE), col),
            vmem,
        ],
        out_specs=(
            pl.BlockSpec((LOCAL, WIDE), col),
            pl.BlockSpec((LOCAL, WIDE), col),
            pl.BlockSpec((WIDE, RANK), lambda i: (i, 0)),
        ),
        compiler_params=pltpu.CompilerParams(vmem_limit_bytes=FINAL_MIB * 1024 * 1024),
    )(moment, change, ortho, right_t, scale)


def local(momentum, gradient, factor):
    new_momentum, step_direction, new_factor = final(momentum[0], gradient[0], *core(momentum[0], gradient[0], factor))
    return new_momentum[None], step_direction, new_factor


def solution(mesh):
    in_specs = (P("dp", "fsdp", "tensor"), P("dp", "fsdp", "tensor"), P("tensor", None))
    out_specs = (P("dp", "fsdp", "tensor"), P("fsdp", "tensor"), P("tensor", None))
    return jax.shard_map(local, mesh=mesh, in_specs=in_specs, out_specs=out_specs, check_vma=False)
```
